512 devices in a mesh: dp: 32 (over z_hi, x, core), tensor: 16 (over z_lo, y).
Axes of the slice: x: 4, y: 4, z: 16 (z_hi: 4, z_lo: 4; z = z_hi * 4 + z_lo), core: 2. Of those that a mesh axis runs over, the one named last changes fastest.
Arguments:
- tokens: bfloat16 [4096, 8192], P('dp', 'tensor'), may hold values from -6 to 6
- cotangent: bfloat16 [4096, 8192], P('dp', 'tensor'), may hold values from -6 to 6
- up_blocks: bfloat16 [5, 64, 128, 256], P(None, 'tensor'), may hold values from -0.15625 to 0.15625
- up_left: bfloat16 [8192, 128], P('tensor'), may hold values from -0.0625 to 0.0625
- up_right: bfloat16 [128, 16384], P(None, 'tensor'), may hold values from -0.375 to 0.375
- down_blocks: bfloat16 [5, 64, 256, 128], P(None, 'tensor'), may hold values from -0.125 to 0.125
- down_left: bfloat16 [16384, 128], P('tensor'), may hold values from -0.046875 to 0.046875
- down_right: bfloat16 [128, 8192], P(None, 'tensor'), may hold values from -0.375 to 0.375
Outputs:
- out: bfloat16 [4096, 8192], P('dp', 'tensor')
- tokens_grad: bfloat16 [4096, 8192], P('dp', 'tensor')
- up_blocks_grad: bfloat16 [5, 64, 128, 256], P(None, 'tensor', 'dp')
- up_left_grad: bfloat16 [8192, 128], P('tensor', 'dp')
- up_right_grad: bfloat16 [128, 16384], P('dp', 'tensor')
- down_blocks_grad: bfloat16 [5, 64, 256, 128], P(None, 'tensor', 'dp')
- down_left_grad: bfloat16 [16384, 128], P('tensor', 'dp')
- down_right_grad: bfloat16 [128, 8192], P('dp', 'tensor')
The draws below stay inside these ranges and needn't reach their ends.
All inputs are finite; a program needn't handle non-finite values.
Results may differ from the reference program's by a relative error of at most 0.03.
Values may be sent and summed in bfloat16 or wider, within the bound.
No kernel may reach another device: no remote copies, remote signals or barrier semaphores. Data moves between devices by JAX's collectives and lax.ppermute only.
A program may use at most 64 MiB of HBM per device.

```python
import math
import jax
import jax.numpy as jnp
import numpy as np
from jax import lax

D = 8192
FF = 16384
BLOCK = 128
R = 128
TOK_DEV = 128
FACTORS = 5
HB = 256
TOKENS = 4096
N_DP = 32
N_TENSOR = 16


def levels(stream_key, dims, split, low, largest):
    factor_of, own = 1.0, jax.random.fold_in(stream_key, 6)
    for axis_at, shards_of in split:
        heights = jnp.exp(jax.random.uniform(jax.random.fold_in(own, axis_at), (shards_of,), jnp.float32, low / len(split), largest / len(split)))
        factor_of = factor_of * jnp.repeat(heights, dims[axis_at] // shards_of).reshape([-1 if axis == axis_at else 1 for axis in range(len(dims))])
    return factor_of


def normal_values(key, shape, scale, bound, cuts=(), dtype=jnp.bfloat16):
    values = scale * jax.random.normal(key, shape, jnp.float32)
    if cuts:
        values = values * levels(key, shape, cuts, -0.22, 0.18)
    return jnp.clip(values, -bound, bound).astype(dtype)


def setup_inputs(seed: int = 0) -> dict:
    seeds = jax.random.split(jax.random.key(seed), 9)
    return {
        "tokens": normal_values(seeds[0], (TOKENS, D), 1.0, 6.0, ((0, 32), (1, 16))),
        "cotangent": normal_values(seeds[1], (TOKENS, D), 1.0, 6.0, ((0, 32), (1, 16))),
        "up_blocks": normal_values(seeds[2], (FACTORS, D // BLOCK, BLOCK, HB), (2 * FACTORS * BLOCK) ** -0.5, 0.15625, ((1, 16),)),
        "up_left": normal_values(seeds[3], (D, R), D ** -0.5, 0.0625, ((0, 16),)),
        "up_right": normal_values(seeds[4], (R, FF), (2 * R) ** -0.5, 0.375, ((1, 16),)),
        "down_blocks": normal_values(seeds[5], (FACTORS, D // BLOCK, HB, BLOCK), (2 * FACTORS * HB) ** -0.5, 0.125, ((1, 16),)),
        "down_left": normal_values(seeds[6], (FF, R), FF ** -0.5, 0.046875, ((0, 16),)),
        "down_right": normal_values(seeds[7], (R, D), (2 * R) ** -0.5, 0.375, ((1, 16),)),
    }


def smooth_gate(values):
    return jax.nn.gelu(values, approximate=False)

def widen(array):
    return array.astype(jnp.float32)

def rounded(array):
    return lax.optimization_barrier(array.astype(jnp.bfloat16)).astype(jnp.float32)

def reference(tokens, cotangent, up_blocks, up_left, up_right, down_blocks, down_left, down_right):
    slab_count = N_TENSOR
    per_slab = D // (BLOCK * N_TENSOR)
    partners = [np.arange(slab_count) ^ (0 if factor == 0 else 1 << factor - 1) for factor in range(FACTORS)]
    up_table = widen(up_blocks).reshape(FACTORS, slab_count, per_slab, BLOCK, HB)
    down_table = widen(down_blocks).reshape(FACTORS, slab_count, per_slab, HB, BLOCK)
    grad_scale = 1.0 / math.sqrt(TOKENS)

    def shard_step(carry, inputs):
        shard_tokens, shard_cot = inputs
        row_count = shard_tokens.shape[0]
        token_slabs = widen(shard_tokens).reshape(row_count, slab_count, per_slab, BLOCK)
        cot_slabs = widen(shard_cot).reshape(row_count, slab_count, per_slab, BLOCK)
        low_up = jnp.dot(shard_tokens, up_left, preferred_element_type=jnp.float32).astype(jnp.bfloat16)
        low_cot = jnp.einsum('nd,rd->nr', widen(shard_cot), widen(down_right)).astype(jnp.bfloat16)
        hidden_pre = jnp.dot(low_up, up_right, preferred_element_type=jnp.float32).reshape(row_count, slab_count, per_slab, HB)
        for factor in range(FACTORS):
            hidden_pre = hidden_pre + jnp.einsum('ntbi,tbih->ntbh', token_slabs[:, partners[factor]], up_table[factor])
        hidden_pre = hidden_pre.reshape(row_count, FF)
        active, gelu_back = jax.vjp(smooth_gate, hidden_pre)
        hidden = active.astype(jnp.bfloat16)
        hidden_slabs = widen(hidden).reshape(row_count, slab_count, per_slab, HB)
        low_down = jnp.dot(hidden, down_left, preferred_element_type=jnp.float32).astype(jnp.bfloat16)
        out_sum = jnp.dot(low_down, down_right, preferred_element_type=jnp.float32).reshape(row_count, slab_count, per_slab, BLOCK)
        for factor in range(FACTORS):
            partial_value = jnp.einsum('nsbh,sbhi->nsbi', hidden_slabs, down_table[factor])
            out_sum = out_sum + partial_value[:, partners[factor]]
        shard_out = out_sum.reshape(row_count, D).astype(jnp.bfloat16)
        hidden_grad = jnp.einsum('nr,hr->nh', widen(low_cot), widen(down_left)).reshape(row_count, slab_count, per_slab, HB)
        for factor in range(FACTORS):
            hidden_grad = hidden_grad + jnp.einsum('nsbi,sbhi->nsbh', cot_slabs[:, partners[factor]], down_table[factor])
        pre_grad = gelu_back(hidden_grad.reshape(row_count, FF))[0].astype(jnp.bfloat16)
        pre_slabs = widen(pre_grad).reshape(row_count, slab_count, per_slab, HB)
        low_pre = jnp.einsum('nh,rh->nr', widen(pre_grad), widen(up_right)).astype(jnp.bfloat16)
        token_sum = jnp.einsum('nr,dr->nd', widen(low_pre), widen(up_left)).reshape(row_count, slab_count, per_slab, BLOCK)
        for factor in range(FACTORS):
            partial_value = jnp.einsum('ntbh,tbih->ntbi', pre_slabs, up_table[factor])
            token_sum = token_sum + partial_value[:, partners[factor]]
        shard_grad = token_sum.reshape(row_count, D).astype(jnp.bfloat16)
        up_terms = jnp.stack([jnp.einsum('ntbi,ntbh->tbih', token_slabs[:, partners[factor]], pre_slabs) for factor in range(FACTORS)])
        down_terms = jnp.stack([jnp.einsum('nsbh,nsbi->sbhi', hidden_slabs, cot_slabs[:, partners[factor]]) for factor in range(FACTORS)])
        terms = (up_terms.reshape(FACTORS, slab_count * per_slab, BLOCK, HB), jnp.einsum('nd,nr->dr', widen(shard_tokens), widen(low_pre)), jnp.einsum('nr,nh->rh', widen(low_up), widen(pre_grad)), down_terms.reshape(FACTORS, slab_count * per_slab, HB, BLOCK), jnp.einsum('nh,nr->hr', widen(hidden), widen(low_cot)), jnp.einsum('nr,nd->rd', widen(low_down), widen(shard_cot)))
        carry = tuple((total + rounded(term * grad_scale) for total, term in zip(carry, terms)))
        return (carry, (shard_out, shard_grad))
    start = (jnp.zeros((FACTORS, D // BLOCK, BLOCK, HB), jnp.float32), jnp.zeros((D, R), jnp.float32), jnp.zeros((R, FF), jnp.float32), jnp.zeros((FACTORS, D // BLOCK, HB, BLOCK), jnp.float32), jnp.zeros((FF, R), jnp.float32), jnp.zeros((R, D), jnp.float32))
    stacked = (tokens.reshape(N_DP, TOK_DEV, D), cotangent.reshape(N_DP, TOK_DEV, D))
    sums, results = lax.scan(shard_step, start, stacked)
    out = results[0].reshape(TOKENS, D)
    tokens_grad = results[1].reshape(TOKENS, D)
    grads = tuple((total.astype(jnp.bfloat16) for total in sums))
    return (out, tokens_grad, grads[0], grads[1], grads[2], grads[3], grads[4], grads[5])
```

```python
import functools
import math

import jax
import jax.numpy as jnp
from jax import lax
from jax.experimental import pallas as pl
from jax.experimental.pallas import tpu as pltpu
from jax.sharding import Mesh
from jax.sharding import PartitionSpec as P

DP = ("zh", "x", "core")
TENSOR = ("zl", "y")
SIZES = (4, 4, 2, 4, 4)
ROWS = 128
SIDE = 256
SLAB = 512
HIDDEN = 1024
BLOCKS = 4
FACTORS = 5
F32 = jnp.float32
BF16 = jnp.bfloat16

GROUP = BLOCKS * SIDE
DOWN_AT = 3 * GROUP
LEFT_AT = DOWN_AT + BLOCKS * FACTORS * ROWS
MAIN = LEFT_AT + SLAB
MINI = SLAB
LIMIT = 48 * 1024 * 1024


def mm(a, b):
    return lax.dot_general(a, b, (((1,), (0,)), ((), ())), preferred_element_type=F32)


def mt(a, b):
    return lax.dot_general(a, b, (((1,), (1,)), ((), ())), preferred_element_type=F32)


def pick(core):
    row = lax.broadcasted_iota(jnp.int32, (SIDE, SIDE), 0)
    column = lax.broadcasted_iota(jnp.int32, (SIDE, SIDE), 1)
    quarter, half = row & 3, (row >> 2) & 1
    zh, x = (row >> 3) & 3, (row >> 5) & 3
    at = (zh * 8 + x * 2) + ((row >> 7) ^ core)
    pair = (column == half * ROWS + at * 4 + quarter).astype(BF16)
    whole = (column == at * 8 + half * 4 + quarter).astype(BF16)
    return pair, whole


def low_body(tokens, cotangent, up_left, down_right, low, both):
    t, c = tokens[...], cotangent[...]
    both[:ROWS, :] = t
    both[ROWS:, :] = c
    low[:, :ROWS] = mm(t, up_left[...])
    low[:, ROWS:] = mt(c, down_right[...])


def main_body(
    scale, core, own, one, two, three, four, low, up, up_right, down, down_left,
    local, out_one, out_two, out_three, out_four, low_next, keep, send,
):
    arrived = (own, one, two, three, four)
    sent = (local, out_one, out_two, out_three, out_four)
    pair, whole = pick(core[0])
    low_up, low_cot = low[:, :ROWS], low[:, ROWS:]

    def put(at, value):
        value = (value * scale).astype(BF16)
        keep[:, at : at + value.shape[1]] = value[:ROWS]
        send[:, at : at + value.shape[1]] = value[ROWS:]

    hidden_parts = []
    low_down = jnp.zeros((ROWS, ROWS), F32)
    low_pre = jnp.zeros((ROWS, ROWS), F32)
    for b in range(BLOCKS):
        features = slice(b * ROWS, (b + 1) * ROWS)
        units = slice(b * SIDE, (b + 1) * SIDE)
        tok = [a[:ROWS, features] for a in arrived]
        cot = [a[ROWS:, features] for a in arrived]
        value = mm(low_up, up_right[:, units])
        grad = mt(low_cot, down_left[units, :])
        for k in range(FACTORS):
            value = value + mm(tok[k], up[k, b])
            grad = grad + mt(cot[k], down[k, b])
        phi = 0.5 + 0.5 * lax.erf(value * math.sqrt(0.5))
        density = jnp.exp(-0.5 * value * value) * (1.0 / math.sqrt(2.0 * math.pi))
        hidden = (value * phi).astype(BF16)
        pre = (grad * (phi + value * density)).astype(BF16)
        hidden_parts.append(hidden)
        for k in range(FACTORS):
            kind = sent[k].dtype
            sent[k][:ROWS, features] = mm(hidden, down[k, b]).astype(kind)
            sent[k][ROWS:, features] = mt(pre, up[k, b]).astype(kind)
        low_down = low_down + mm(hidden, down_left[units, :])
        low_pre = low_pre + mt(pre, up_right[:, units])
        left = tok + [low_up]
        for g in range(3):
            rows = jnp.concatenate([left[2 * g], left[2 * g + 1]], axis=1)
            put(g * GROUP + b * SIDE, mm(mt(pair, rows).astype(BF16), pre))
        rows = mt(whole, hidden).astype(BF16)
        put(DOWN_AT + b * FACTORS * ROWS, mm(rows, jnp.concatenate(cot, axis=1)))
    low_next[:, :ROWS] = low_down
    low_next[:, ROWS:] = low_pre
    zero = jnp.zeros_like(low_cot)
    upper = mt(pair, jnp.concatenate([low_cot, zero], axis=1)).astype(BF16)
    lower = mt(pair, jnp.concatenate([zero, low_cot], axis=1)).astype(BF16)
    put(
        LEFT_AT,
        mm(upper, jnp.concatenate(hidden_parts[:2], axis=1))
        + mm(lower, jnp.concatenate(hidden_parts[2:], axis=1)),
    )


def mini_body(scale, core, own, low, keep, send):
    pair, _ = pick(core[0])
    low_down, low_pre = low[:, :ROWS], low[:, ROWS:]
    zero = jnp.zeros_like(low_pre)
    upper = mt(pair, jnp.concatenate([low_pre, zero], axis=1)).astype(BF16)
    lower = mt(pair, jnp.concatenate([zero, low_down], axis=1)).astype(BF16)
    value = ((mm(upper, own[:ROWS, :]) + mm(lower, own[ROWS:, :])) * scale).astype(BF16)
    keep[...] = value[:ROWS]
    send[...] = value[ROWS:]


def last_body(local, one, two, three, four, low, up_left, down_right, out, grad):
    total = local[...]
    for a in (one, two, three, four):
        total = total + a[...].astype(F32)
    out[...] = (total[:ROWS] + mm(low[:, :ROWS], down_right[...])).astype(BF16)
    grad[...] = (total[ROWS:] + mt(low[:, ROWS:], up_left[...])).astype(BF16)


def unpack_body(parts, up, up_left, up_right, down, down_left, down_right):
    total = parts[0].astype(F32)
    for z in range(1, parts.shape[0]):
        total = total + parts[z].astype(F32)
    top, low = total[:4].astype(BF16), total[4:].astype(BF16)
    total = total.astype(BF16)
    for b in range(BLOCKS):
        for k in range(FACTORS):
            at = (k // 2) * GROUP + b * SIDE
            up[k, b] = (low if k % 2 else top)[:, at : at + SIDE]
            at = DOWN_AT + (b * FACTORS + k) * ROWS
            down[k, b] = total[:, at : at + ROWS]
    up_right[...] = low[:, 2 * GROUP : 3 * GROUP]
    down_left[:, :SLAB] = top[:, LEFT_AT:MAIN]
    down_left[:, SLAB:] = low[:, LEFT_AT:MAIN]
    up_left[...] = top[:, MAIN:]
    down_right[...] = low[:, MAIN:]


def call(body, outs, scalars=0, cost=(0, 0)):
    vmem = pl.BlockSpec(memory_space=pltpu.VMEM)
    smem = pl.BlockSpec(memory_space=pltpu.SMEM)

    def run(*args):
        return pl.pallas_call(
            body,
            out_shape=[jax.ShapeDtypeStruct(s, d) for s, d in outs],
            in_specs=[smem] * scalars + [vmem] * (len(args) - scalars),
            out_specs=[vmem] * len(outs),
            compiler_params=pltpu.CompilerParams(vmem_limit_bytes=LIMIT),
            cost_estimate=pl.CostEstimate(
                flops=cost[0], bytes_accessed=cost[1], transcendentals=0
            ),
        )(*args)

    return run


def swap(block, axis, mask):
    count = lax.axis_size(axis)
    return lax.ppermute(block, axis, [(i, i ^ mask) for i in range(count)])


def all_sum(partial):
    count = SIZES[3] * SIZES[4]
    pieces = partial.reshape(count, ROWS // count, 2 * ROWS)
    pieces = lax.all_to_all(pieces, TENSOR, 0, 0)
    piece = jnp.sum(pieces, axis=0).astype(BF16)
    pieces = jnp.broadcast_to(piece, pieces.shape)
    return lax.all_to_all(pieces, TENSOR, 0, 0).reshape(ROWS, 2 * ROWS)


def add(a, b):
    return (a.astype(F32) + b.astype(F32)).astype(BF16)


def over_x(block):
    pieces = block.reshape(SIZES[1], -1, block.shape[1])
    pieces = lax.all_to_all(pieces, "x", 0, 0)
    return jnp.sum(pieces.astype(F32), axis=0).astype(BF16)


def body(tokens, cotangent, up_blocks, up_left, up_right, down_blocks, down_left, down_right):
    scale = 1.0 / math.sqrt(ROWS * SIZES[0] * SIZES[1] * SIZES[2])
    core = lax.axis_index("core").astype(jnp.int32).reshape(1)
    wide = (2 * ROWS, SLAB)
    hops = (("y", 1), ("y", 2), ("zl", 1), ("zl", 2))

    low, own = call(
        low_body, [((ROWS, 2 * ROWS), F32), (wide, BF16)], cost=(40_000_000, 1_000_000)
    )(tokens, cotangent, up_left, down_right)
    arrived = [swap(own, axis, mask) for axis, mask in hops]
    low = all_sum(low)

    half = (ROWS, MAIN)
    local, *terms, low_next, keep, send = call(
        functools.partial(main_body, scale),
        [(wide, F32)] + [(wide, BF16)] * 4 + [((ROWS, 2 * ROWS), F32), (half, BF16), (half, BF16)],
        scalars=1,
        cost=(1_500_000_000, 10_000_000),
    )(core, own, *arrived, low, up_blocks, up_right, down_blocks, down_left)

    reduced = over_x(add(keep, swap(send, "core", 1)))
    terms = [swap(term, axis, mask) for term, (axis, mask) in zip(terms, hops)]
    low_next = all_sum(low_next)

    half = (ROWS, MINI)
    keep, send = call(
        functools.partial(mini_body, scale), [(half, BF16)] * 2, scalars=1, cost=(40_000_000, 1_000_000)
    )(core, own, low_next)
    mini = over_x(add(keep, swap(send, "core", 1)))

    out, tokens_grad = call(
        last_body, [((ROWS, SLAB), BF16)] * 2, cost=(40_000_000, 2_000_000)
    )(local, *terms, low_next, up_left, down_right)

    pieces = jnp.concatenate([reduced, mini], axis=1).reshape(SIZES[0], 8, MAIN + MINI)
    pieces = lax.all_to_all(pieces, "zh", 0, 0)
    up_g, up_left_g, up_right_g, down_g, down_left_g, down_right_g = call(
        unpack_body,
        [
            ((FACTORS, BLOCKS, 4, SIDE), BF16),
            ((4, SLAB), BF16),
            ((4, HIDDEN), BF16),
            ((FACTORS, BLOCKS, 8, ROWS), BF16),
            ((4, HIDDEN), BF16),
            ((4, SLAB), BF16),
        ],
        cost=(1_000_000, 1_000_000),
    )(pieces)
    return (out, tokens_grad, up_g, up_left_g.T, up_right_g, down_g, down_left_g.T, down_right_g)


def solution(mesh):
    fine = Mesh(mesh.devices.reshape(SIZES), DP + TENSOR)
    in_specs = (
        P(DP, TENSOR),
        P(DP, TENSOR),
        P(None, TENSOR, None, None),
        P(TENSOR, None),
        P(None, TENSOR),
        P(None, TENSOR, None, None),
        P(TENSOR, None),
        P(None, TENSOR),
    )
    out_specs = (
        P(DP, TENSOR),
        P(DP, TENSOR),
        P(None, TENSOR, DP, None),
        P(TENSOR, DP),
        P(DP, TENSOR),
        P(None, TENSOR, DP, None),
        P(TENSOR, DP),
        P(DP, TENSOR),
    )
    return jax.shard_map(body, mesh=fine, in_specs=in_specs, out_specs=out_specs, check_vma=False)
```

```python
import functools
import math

import jax
import jax.numpy as jnp
from jax import lax
from jax.experimental import pallas as pl
from jax.experimental.pallas import tpu as pltpu
from jax.sharding import Mesh
from jax.sharding import PartitionSpec as P

DP = ("zh", "x", "core")
TENSOR = ("zl", "y")
SIZES = (4, 4, 2, 4, 4)
ROWS = 128
SIDE = 256
SLAB = 512
HIDDEN = 1024
BLOCKS = 4
FACTORS = 5
F32 = jnp.float32
BF16 = jnp.bfloat16

GROUP = BLOCKS * SIDE
DOWN_AT = 3 * GROUP
LEFT_AT = DOWN_AT + BLOCKS * FACTORS * ROWS
MAIN = LEFT_AT + SLAB
MINI = SLAB
LOW = ROWS // 2
LIMIT = 24 * 1024 * 1024


def mm(a, b):
    return lax.dot_general(a, b, (((1,), (0,)), ((), ())), preferred_element_type=F32)


def mt(a, b):
    return lax.dot_general(a, b, (((1,), (1,)), ((), ())), preferred_element_type=F32)


def pick(place):
    core, x_here, z_here = place[0], place[2], place[3]
    row = lax.broadcasted_iota(jnp.int32, (SIDE, SIDE), 0)
    column = lax.broadcasted_iota(jnp.int32, (SIDE, SIDE), 1)
    quarter, half = row & 3, (row >> 2) & 1
    zh, x = (row >> 3) & 3, (row >> 5) & 3
    at = (zh ^ z_here) * 8 + (x ^ x_here) * 2 + ((row >> 7) ^ core)
    pair = (column == half * ROWS + at * 4 + quarter).astype(BF16)
    whole = (column == at * 8 + half * 4 + quarter).astype(BF16)
    return pair, whole


def pick_mini():
    row = lax.broadcasted_iota(jnp.int32, (SIDE, SIDE), 0)
    column = lax.broadcasted_iota(jnp.int32, (SIDE, SIDE), 1)
    quarter, half = row & 3, (row >> 2) & 1
    at = ((row >> 3) & 3) * 8 + (row >> 5)
    return (column == half * ROWS + at * 4 + quarter).astype(BF16)


class Copies:
    def __init__(self, sems):
        self.sems, self.count = sems, 0

    def start(self, source, target):
        copy = pltpu.make_async_copy(source, target, self.sems.at[self.count])
        self.count += 1
        copy.start()
        return copy


def finish(copies):
    for copy in copies:
        copy.wait()


def fold(low):
    return jnp.concatenate([low[:LOW], low[LOW:]], axis=1).astype(BF16)


def unfold(pieces):
    total = pieces[0].astype(F32)
    for n in range(1, 4):
        total = total + pieces[n].astype(F32)
    total = total.astype(BF16)
    first = jnp.concatenate([total[:, :ROWS], total[:, 2 * ROWS : 3 * ROWS]], axis=0)
    second = jnp.concatenate([total[:, ROWS : 2 * ROWS], total[:, 3 * ROWS :]], axis=0)
    return first, second


def low_body(tokens, cotangent, up_left, down_right, own, packed, both, low, u, d, sems):
    copies = Copies(sems)
    t, c = both.at[:ROWS], both.at[ROWS:]
    first = [copies.start(tokens, t), copies.start(up_left, u)]
    second = [copies.start(cotangent, c), copies.start(down_right, d)]
    finish(first)
    low_up = mm(t[...], u[...])
    finish(second)
    sent = [copies.start(both, own)]
    sent += [copies.start(both, packed.at[n, : 2 * ROWS]) for n in range(4)]
    low_cot = mt(c[...], d[...])
    low[...] = fold(jnp.concatenate([low_up, low_cot], axis=1))
    sent += [copies.start(low, packed.at[n, 2 * ROWS :]) for n in range(4)]
    finish(sent)


def spread_body(near, out, pieces, total, sems):
    copies = Copies(sems)
    copies.start(near.at[:, 2 * ROWS :], pieces).wait()
    value = pieces[0].astype(F32)
    for n in range(1, 4):
        value = value + pieces[n].astype(F32)
    total[...] = value.astype(BF16)
    finish([copies.start(total, out.at[n]) for n in range(4)])


def main_body(
    scale, place, near_hbm, three_hbm, four_hbm, low_hbm, up_hbm, up_right_hbm, down_hbm, down_left_hbm,
    local_out, packed_out, three_out, four_out, keep_out, send_out,
    arrived, low, up, up_right, down, down_left, local, sent, low_next, keep, send, sems,
):
    copies = Copies(sems)
    y = place[1]
    wide = slice(0, 2 * ROWS)
    first = [
        copies.start(low_hbm, low),
        copies.start(up_right_hbm, up_right),
        copies.start(down_left_hbm, down_left),
        copies.start(near_hbm.at[y, wide], arrived.at[0]),
        copies.start(near_hbm.at[y ^ 1, wide], arrived.at[1]),
        copies.start(near_hbm.at[y ^ 2, wide], arrived.at[2]),
        copies.start(three_hbm, arrived.at[3]),
        copies.start(four_hbm, arrived.at[4]),
    ]
    blocks = [
        (copies.start(up_hbm.at[:, b], up.at[:, b]), copies.start(down_hbm.at[:, b], down.at[:, b]))
        for b in range(BLOCKS)
    ]
    pair, whole = pick(place)
    out_going = []

    def put(at, value):
        value = (value * scale).astype(BF16)
        columns = slice(at, at + value.shape[1])
        keep[:, columns] = value[:ROWS]
        send[:, columns] = value[ROWS:]
        out_going.append(copies.start(send.at[:, columns], send_out.at[:, columns]))
        out_going.append(copies.start(keep.at[:, columns], keep_out.at[:, columns]))

    finish(first)
    low_up, low_cot = unfold(low)
    hiddens, pres = [], []
    low_down = jnp.zeros((ROWS, ROWS), F32)
    low_pre = jnp.zeros((ROWS, ROWS), F32)
    for b in range(BLOCKS):
        features = slice(b * ROWS, (b + 1) * ROWS)
        units = slice(b * SIDE, (b + 1) * SIDE)
        tok = [arrived[k, :ROWS, features] for k in range(FACTORS)]
        cot = [arrived[k, ROWS:, features] for k in range(FACTORS)]
        value = mm(low_up, up_right[:, units])
        grad = mt(low_cot, down_left[units, :])
        finish(blocks[b])
        for k in range(FACTORS):
            value = value + mm(tok[k], up[k, b])
            grad = grad + mt(cot[k], down[k, b])
        phi = 0.5 + 0.5 * lax.erf(value * math.sqrt(0.5))
        density = jnp.exp(-0.5 * value * value) * (1.0 / math.sqrt(2.0 * math.pi))
        hidden = (value * phi).astype(BF16)
        pre = (grad * (phi + value * density)).astype(BF16)
        hiddens.append(hidden)
        pres.append(pre)
        left = tok + [low_up]
        for g in range(3):
            rows = jnp.concatenate([left[2 * g], left[2 * g + 1]], axis=1)
            put(g * GROUP + b * SIDE, mm(mt(pair, rows).astype(BF16), pre))
        rows = mt(whole, hidden).astype(BF16)
        put(DOWN_AT + b * FACTORS * ROWS, mm(rows, jnp.concatenate(cot, axis=1)))
    zero = jnp.zeros_like(low_cot)
    upper = mt(pair, jnp.concatenate([low_cot, zero], axis=1)).astype(BF16)
    lower = mt(pair, jnp.concatenate([zero, low_cot], axis=1)).astype(BF16)
    put(
        LEFT_AT,
        mm(upper, jnp.concatenate(hiddens[:2], axis=1))
        + mm(lower, jnp.concatenate(hiddens[2:], axis=1)),
    )
    for b in range(BLOCKS):
        features = slice(b * ROWS, (b + 1) * ROWS)
        units = slice(b * SIDE, (b + 1) * SIDE)
        hidden, pre = hiddens[b], pres[b]
        low_down = low_down + mm(hidden, down_left[units, :])
        low_pre = low_pre + mt(pre, up_right[:, units])
        for k in range(FACTORS):
            upper, lower = mm(hidden, down[k, b]), mt(pre, up[k, b])
            if k:
                sent[k - 1, :ROWS, features] = upper.astype(BF16)
                sent[k - 1, ROWS:, features] = lower.astype(BF16)
            else:
                local[:ROWS, features] = upper
                local[ROWS:, features] = lower
    low_next[...] = fold(jnp.concatenate([low_down, low_pre], axis=1))
    out_going += [
        copies.start(sent.at[0], packed_out.at[y ^ 1, wide]),
        copies.start(sent.at[1], packed_out.at[y ^ 2, wide]),
        copies.start(sent.at[2], three_out),
        copies.start(sent.at[3], four_out),
        copies.start(local, local_out),
    ]
    out_going += [copies.start(sent.at[0], packed_out.at[y, wide])]
    out_going += [copies.start(sent.at[1], packed_out.at[y ^ 3, wide])]
    out_going += [copies.start(low_next, packed_out.at[n, 2 * ROWS :]) for n in range(4)]
    finish(out_going)


def mini_body(scale, own_hbm, pieces_hbm, low, mini, own, pieces, sems):
    copies = Copies(sems)
    first = [copies.start(pieces_hbm, pieces), copies.start(own_hbm, own)]
    pair = pick_mini()
    finish(first)
    low_down, low_pre = unfold(pieces)
    low[:, :ROWS] = low_down
    low[:, ROWS:] = low_pre
    zero = jnp.zeros_like(low_pre)
    upper = mt(pair, jnp.concatenate([low_pre, zero], axis=1)).astype(BF16)
    lower = mt(pair, jnp.concatenate([zero, low_down], axis=1)).astype(BF16)
    value = mm(upper, own[:ROWS, :]) + mm(lower, own[ROWS:, :])
    mini[...] = (value * scale).astype(BF16)


def last_body(
    place, local_hbm, near, three, four, low_hbm, up_left_hbm, down_right_hbm, out, grad,
    local, terms, low, up_left, down_right, sems,
):
    copies = Copies(sems)
    y = place[1]
    wide = slice(0, 2 * ROWS)
    finish([
        copies.start(local_hbm, local),
        copies.start(near.at[y ^ 1, wide], terms.at[0]),
        copies.start(near.at[y ^ 2, wide], terms.at[1]),
        copies.start(three, terms.at[2]),
        copies.start(four, terms.at[3]),
        copies.start(low_hbm, low),
        copies.start(up_left_hbm, up_left),
        copies.start(down_right_hbm, down_right),
    ])
    total = local[...]
    for n in range(4):
        total = total + terms[n].astype(F32)
    out[...] = (total[:ROWS] + mm(low[:, :ROWS], down_right[...])).astype(BF16)
    grad[...] = (total[ROWS:] + mt(low[:, ROWS:], up_left[...])).astype(BF16)


def split_body(a, b, *outs):
    rows = a.shape[0] // len(outs)
    for n, out in enumerate(outs):
        part = slice(n * rows, (n + 1) * rows)
        out[...] = (a[part, :].astype(F32) + b[part, :].astype(F32)).astype(BF16)


def join_body(a, b, c, d, *outs):
    rows = a.shape[0] // len(outs)
    for n, out in enumerate(outs):
        part = slice(n * rows, (n + 1) * rows)
        total = a[part, :].astype(F32) + b[part, :].astype(F32)
        total = total + c[part, :].astype(F32) + d[part, :].astype(F32)
        out[...] = total.astype(BF16)


def unpack_body(one, two, three, four, mini, up, up_left, up_right, down, down_left, down_right):
    total, small = one[...].astype(F32), mini[0].astype(F32)
    for part in (two, three, four):
        total = total + part[...].astype(F32)
    for z in range(1, mini.shape[0]):
        small = small + mini[z].astype(F32)
    top, low = total[:4].astype(BF16), total[4:].astype(BF16)
    total = total.astype(BF16)
    for b in range(BLOCKS):
        for k in range(FACTORS):
            at = (k // 2) * GROUP + b * SIDE
            up[k, b] = (low if k % 2 else top)[:, at : at + SIDE]
            at = DOWN_AT + (b * FACTORS + k) * ROWS
            down[k, b] = total[:, at : at + ROWS]
    up_right[...] = low[:, 2 * GROUP : 3 * GROUP]
    down_left[:, :SLAB] = top[:, LEFT_AT:MAIN]
    down_left[:, SLAB:] = low[:, LEFT_AT:MAIN]
    up_left[...] = small[:4].astype(BF16)
    down_right[...] = small[4:].astype(BF16)


SPACES = {"s": pltpu.SMEM, "v": pltpu.VMEM, "h": pltpu.HBM, "a": pl.ANY}


def call(body, outs, kinds, scratch=(), copies=0, cost=(0, 0)):
    kinds, kinds_out = kinds.split()
    sems = [pltpu.SemaphoreType.DMA((copies,))] if copies else []

    def run(*args):
        args = [
            pltpu.with_memory_space_constraint(a, pltpu.HBM) if k == "h" else a
            for a, k in zip(args, kinds)
        ]
        return pl.pallas_call(
            body,
            out_shape=[jax.ShapeDtypeStruct(s, d) for s, d in outs],
            in_specs=[pl.BlockSpec(memory_space=SPACES[k]) for k in kinds],
            out_specs=[pl.BlockSpec(memory_space=SPACES[k]) for k in kinds_out],
            scratch_shapes=[pltpu.VMEM(s, d) for s, d in scratch] + sems,
            compiler_params=pltpu.CompilerParams(vmem_limit_bytes=LIMIT),
            cost_estimate=pl.CostEstimate(
                flops=cost[0], bytes_accessed=cost[1], transcendentals=0
            ),
        )(*args)

    return run


def in_columns(body, rows_in, rows_out, width, steps, flops=1_000_000):
    spec = lambda rows: pl.BlockSpec((rows, width // steps), lambda i: (0, i))
    return pl.pallas_call(
        body,
        out_shape=[jax.ShapeDtypeStruct((rows, width), BF16) for rows in rows_out],
        grid=(steps,),
        in_specs=[spec(rows) for rows in rows_in],
        out_specs=[spec(rows) for rows in rows_out],
        compiler_params=pltpu.CompilerParams(vmem_limit_bytes=LIMIT),
        cost_estimate=pl.CostEstimate(flops=flops, bytes_accessed=4_000_000, transcendentals=0),
    )


def spread(packed):
    shape = (4, LOW, SLAB)
    return call(
        spread_body, [(shape, BF16)], "a a", [(shape, BF16), (shape[1:], BF16)], 5, cost=(1_000_000, 500_000)
    )(packed)[0]


def swap(block, axis, mask):
    count = lax.axis_size(axis)
    return lax.ppermute(block, axis, [(i, i ^ mask) for i in range(count)])


def exchange(block, axis):
    return lax.all_to_all(block, axis, 0, 0)


def add(a, b):
    return (a.astype(F32) + b.astype(F32)).astype(BF16)


def total_of(pieces):
    return jnp.sum(pieces.astype(F32), axis=0).astype(BF16)


def body(tokens, cotangent, up_blocks, up_left, up_right, down_blocks, down_left, down_right):
    scale = 1.0 / math.sqrt(ROWS * SIZES[0] * SIZES[1] * SIZES[2])
    index = lax.axis_index
    place = jnp.stack([index("core"), index("y"), index("x"), index("zh")]).astype(jnp.int32)
    wide, chunks = (2 * ROWS, SLAB), (4, 2 * ROWS + LOW, SLAB)
    shape = lambda a: (a.shape, a.dtype)

    own, packed = call(
        low_body,
        [(wide, BF16), (chunks, BF16)],
        "hhhh aa",
        [(wide, BF16), ((LOW, SLAB), BF16), shape(up_left), shape(down_right)],
        13,
        cost=(40_000_000, 2_000_000),
    )(tokens, cotangent, up_left, down_right)
    near = exchange(packed, "y")
    far = [swap(own, "zl", mask) for mask in (1, 2)]
    low = exchange(spread(near), "zl")

    half = (ROWS, MAIN)
    weights = (up_blocks, up_right, down_blocks, down_left)
    local, packed, *far, keep, send = call(
        functools.partial(main_body, scale),
        [(wide, F32), (chunks, BF16), (wide, BF16), (wide, BF16), (half, BF16), (half, BF16)],
        "saaaahhhh aaaaaa",
        [((FACTORS, *wide), BF16), shape(low)]
        + [shape(a) for a in weights]
        + [(wide, F32), ((FACTORS - 1, *wide), BF16), ((LOW, SLAB), BF16), (half, BF16), (half, BF16)],
        64,
        cost=(1_500_000_000, 10_000_000),
    )(place, near, *far, low, *weights)

    got = swap(send, "core", 1)
    pieces = in_columns(split_body, [ROWS] * 2, [32] * 4, MAIN, 4)(keep, got)
    packed, far, pieces = lax.optimization_barrier((packed, far, pieces))
    pieces = list(pieces[:1]) + [swap(pieces[mask], "x", mask) for mask in (1, 2, 3)]
    far = [swap(term, "zl", mask) for term, mask in zip(far, (1, 2))]
    near = exchange(packed, "y")
    low = exchange(spread(near), "zl")

    pieces, far = lax.optimization_barrier((pieces, far))
    pieces = in_columns(join_body, [32] * 4, [8] * 4, MAIN, 2, 30_000_000_000)(*pieces)
    low, pieces = lax.optimization_barrier((low, pieces))
    pieces = list(pieces[:1]) + [swap(pieces[mask], "zh", mask) for mask in (1, 2, 3)]

    low, mini = call(
        functools.partial(mini_body, scale),
        [((ROWS, 2 * ROWS), BF16), ((2 * ROWS, MINI), BF16)],
        "aa vv",
        [shape(own), shape(low)],
        2,
        cost=(40_000_000, 1_000_000),
    )(own, low)
    mini = total_of(exchange(mini.reshape(8, -1, MINI), ("x", "core")))
    mini = exchange(mini.reshape(SIZES[0], 8, MINI), "zh")

    out, tokens_grad = call(
        last_body,
        [((ROWS, SLAB), BF16)] * 2,
        "saaaaahh vv",
        [(wide, F32), ((4, *wide), BF16), shape(low), shape(up_left), shape(down_right)],
        8,
        cost=(40_000_000, 2_000_000),
    )(place, local, near, *far, low, up_left, down_right)

    up_g, up_left_g, up_right_g, down_g, down_left_g, down_right_g = call(
        unpack_body,
        [
            ((FACTORS, BLOCKS, 4, SIDE), BF16),
            ((4, SLAB), BF16),
            ((4, HIDDEN), BF16),
            ((FACTORS, BLOCKS, 8, ROWS), BF16),
            ((4, HIDDEN), BF16),
            ((4, SLAB), BF16),
        ],
        "vvvvv vvvvvv",
        cost=(1_000_000, 1_000_000),
    )(*pieces, mini)
    return (out, tokens_grad, up_g, up_left_g.T, up_right_g, down_g, down_left_g.T, down_right_g)


def solution(mesh):
    fine = Mesh(mesh.devices.reshape(SIZES), DP + TENSOR)
    in_specs = (
        P(DP, TENSOR),
        P(DP, TENSOR),
        P(None, TENSOR, None, None),
        P(TENSOR, None),
        P(None, TENSOR),
        P(None, TENSOR, None, None),
        P(TENSOR, None),
        P(None, TENSOR),
    )
    out_specs = (
        P(DP, TENSOR),
        P(DP, TENSOR),
        P(None, TENSOR, DP, None),
        P(TENSOR, DP),
        P(DP, TENSOR),
        P(None, TENSOR, DP, None),
        P(TENSOR, DP),
        P(DP, TENSOR),
    )
    return jax.shard_map(body, mesh=fine, in_specs=in_specs, out_specs=out_specs, check_vma=False)
```

```python
import functools
import math

import jax
import jax.numpy as jnp
from jax import lax
from jax.experimental import pallas as pl
from jax.experimental.pallas import tpu as pltpu
from jax.sharding import Mesh
from jax.sharding import PartitionSpec as P

DP = ("zh", "x", "core")
TENSOR = ("zl", "y")
SIZES = (4, 4, 2, 4, 4)
ROWS = 128
SIDE = 256
SLAB = 512
HIDDEN = 1024
BLOCKS = 4
FACTORS = 5
F32 = jnp.float32
BF16 = jnp.bfloat16

GROUP = BLOCKS * SIDE
DOWN_AT = 3 * GROUP
LEFT_AT = DOWN_AT + BLOCKS * FACTORS * ROWS
MAIN = LEFT_AT + SLAB
MINI = SLAB
LOW = ROWS // 2
LIMIT = 63 * 1024 * 1024
SMALL = 16 * 1024 * 1024


def mm(a, b):
    return lax.dot_general(a, b, (((1,), (0,)), ((), ())), preferred_element_type=F32)


def mt(a, b):
    return lax.dot_general(a, b, (((1,), (1,)), ((), ())), preferred_element_type=F32)


def pick(place):
    core, x_here = place[0], place[1]
    row = lax.broadcasted_iota(jnp.int32, (SIDE, SIDE), 0)
    column = lax.broadcasted_iota(jnp.int32, (SIDE, SIDE), 1)
    quarter, half = row & 3, (row >> 2) & 1
    zh, x = (row >> 3) & 3, (row >> 5) & 3
    at = zh * 8 + (x ^ x_here) * 2 + ((row >> 7) ^ core)
    pair = (column == half * ROWS + at * 4 + quarter).astype(BF16)
    whole = (column == at * 8 + half * 4 + quarter).astype(BF16)
    return pair, whole


def pick_mini():
    row = lax.broadcasted_iota(jnp.int32, (SIDE, SIDE), 0)
    column = lax.broadcasted_iota(jnp.int32, (SIDE, SIDE), 1)
    quarter, half = row & 3, (row >> 2) & 1
    at = ((row >> 3) & 3) * 8 + (row >> 5)
    return (column == half * ROWS + at * 4 + quarter).astype(BF16)


class Copies:
    def __init__(self, sems):
        self.sems, self.count = sems, 0

    def start(self, source, target):
        copy = pltpu.make_async_copy(source, target, self.sems.at[self.count])
        self.count += 1
        copy.start()
        return copy


def finish(copies):
    for copy in copies:
        copy.wait()


def fold(low):
    return jnp.concatenate([low[:LOW], low[LOW:]], axis=1).astype(BF16)


def unfold(pieces):
    total = pieces[0].astype(F32)
    for n in range(1, pieces.shape[0]):
        total = total + pieces[n].astype(F32)
    total = total.astype(BF16)
    first = jnp.concatenate([total[:, :ROWS], total[:, 2 * ROWS : 3 * ROWS]], axis=0)
    second = jnp.concatenate([total[:, ROWS : 2 * ROWS], total[:, 3 * ROWS :]], axis=0)
    return first, second


def low_body(tokens, cotangent, up_left, down_right, own, low, u, d, sems):
    copies = Copies(sems)
    t, c = own.at[:ROWS], own.at[ROWS:]
    first = [copies.start(tokens, t), copies.start(up_left, u)]
    second = [copies.start(cotangent, c), copies.start(down_right, d)]
    finish(first)
    low[:, :ROWS] = mm(t[...], u[...])
    finish(second)
    low[:, ROWS:] = mt(c[...], d[...])


def main_body(
    scale, place, own_at, one_at, two_at, three_at, four_at, low_at, up_at, up_right_at, down_at, down_left_at,
    local_to, one_to, two_to, three_to, four_to, packed_to, keep_to, send_to,
    arrived, low, up, up_right, down, down_left, local, sent, packed, keep, send, sems,
):
    copies = Copies(sems)
    first = [
        copies.start(low_at, low),
        copies.start(up_right_at, up_right),
        copies.start(down_left_at, down_left),
    ]
    first += [
        copies.start(a, arrived.at[n])
        for n, a in enumerate((own_at, one_at, two_at, three_at, four_at))
    ]
    blocks = [
        (copies.start(up_at.at[:, b], up.at[:, b]), copies.start(down_at.at[:, b], down.at[:, b]))
        for b in range(BLOCKS)
    ]
    pair, whole = pick(place)
    out_going = []

    def put(at, value):
        value = (value * scale).astype(BF16)
        columns = slice(at, at + value.shape[1])
        keep[:, columns] = value[:ROWS]
        send[:, columns] = value[ROWS:]
        out_going.append(copies.start(send.at[:, columns], send_to.at[:, columns]))
        out_going.append(copies.start(keep.at[:, columns], keep_to.at[:, columns]))

    finish(first)
    low_up, low_cot = low[:, :ROWS], low[:, ROWS:]
    hiddens, pres = [], []
    low_down = jnp.zeros((ROWS, ROWS), F32)
    low_pre = jnp.zeros((ROWS, ROWS), F32)
    for b in range(BLOCKS):
        features = slice(b * ROWS, (b + 1) * ROWS)
        units = slice(b * SIDE, (b + 1) * SIDE)
        value = mm(low_up, up_right[:, units])
        grad = mt(low_cot, down_left[units, :])
        finish(blocks[b])
        for k in range(FACTORS):
            value = value + mm(arrived[k, :ROWS, features], up[k, b])
            grad = grad + mt(arrived[k, ROWS:, features], down[k, b])
        phi = 0.5 + 0.5 * lax.erf(value * math.sqrt(0.5))
        density = jnp.exp(-0.5 * value * value) * (1.0 / math.sqrt(2.0 * math.pi))
        hidden = (value * phi).astype(BF16)
        pre = (grad * (phi + value * density)).astype(BF16)
        hiddens.append(hidden)
        pres.append(pre)
        low_down = low_down + mm(hidden, down_left[units, :])
        low_pre = low_pre + mt(pre, up_right[:, units])
    packed[...] = fold(jnp.concatenate([low_down, low_pre], axis=1))
    out_going += [copies.start(packed, packed_to.at[n]) for n in range(packed_to.shape[0])]
    for b in range(BLOCKS):
        features = slice(b * ROWS, (b + 1) * ROWS)
        hidden, pre = hiddens[b], pres[b]
        for k in range(FACTORS):
            upper, lower = mm(hidden, down[k, b]), mt(pre, up[k, b])
            if k:
                sent[k - 1, :ROWS, features] = upper.astype(BF16)
                sent[k - 1, ROWS:, features] = lower.astype(BF16)
            else:
                local[:ROWS, features] = upper
                local[ROWS:, features] = lower
    for n, to in enumerate((one_to, two_to, three_to, four_to)):
        out_going.append(copies.start(sent.at[n], to))
    out_going.append(copies.start(local, local_to))
    for b in range(BLOCKS):
        features = slice(b * ROWS, (b + 1) * ROWS)
        hidden, pre = hiddens[b], pres[b]
        left = [arrived[k, :ROWS, features] for k in range(FACTORS)] + [low_up]
        cot = [arrived[k, ROWS:, features] for k in range(FACTORS)]
        for g in range(3):
            rows = jnp.concatenate([left[2 * g], left[2 * g + 1]], axis=1)
            put(g * GROUP + b * SIDE, mm(mt(pair, rows).astype(BF16), pre))
        rows = mt(whole, hidden).astype(BF16)
        put(DOWN_AT + b * FACTORS * ROWS, mm(rows, jnp.concatenate(cot, axis=1)))
    zero = jnp.zeros_like(low_cot)
    upper = mt(pair, jnp.concatenate([low_cot, zero], axis=1)).astype(BF16)
    lower = mt(pair, jnp.concatenate([zero, low_cot], axis=1)).astype(BF16)
    put(
        LEFT_AT,
        mm(upper, jnp.concatenate(hiddens[:2], axis=1))
        + mm(lower, jnp.concatenate(hiddens[2:], axis=1)),
    )
    finish(out_going)


def mini_body(scale, own, pieces, low, mini):
    pair = pick_mini()
    low_down, low_pre = unfold(pieces)
    low[:, :ROWS] = low_down
    low[:, ROWS:] = low_pre
    zero = jnp.zeros_like(low_pre)
    upper = mt(pair, jnp.concatenate([low_pre, zero], axis=1)).astype(BF16)
    lower = mt(pair, jnp.concatenate([zero, low_down], axis=1)).astype(BF16)
    value = mm(upper, own[:ROWS, :]) + mm(lower, own[ROWS:, :])
    mini[...] = (value * scale).astype(BF16)


def last_body(local, one, two, three, four, low, up_left, down_right, out, grad):
    total = local[...]
    for a in (one, two, three, four):
        total = total + a[...].astype(F32)
    out[...] = (total[:ROWS] + mm(low[:, :ROWS], down_right[...])).astype(BF16)
    grad[...] = (total[ROWS:] + mt(low[:, ROWS:], up_left[...])).astype(BF16)


STEPS = 4


def columns_of(n):
    return slice(n * (MAIN // STEPS), (n + 1) * (MAIN // STEPS))


def split_body(a_at, b_at, one_to, two_to, three_to, four_to, a, b, sems):
    copies = Copies(sems)
    coming = [
        [copies.start(at.at[:, columns_of(n)], to.at[:, columns_of(n)]) for at, to in ((a_at, a), (b_at, b))]
        for n in range(STEPS)
    ]
    going = []
    for n in range(STEPS):
        part = columns_of(n)
        finish(coming[n])
        a[:, part] = (a[:, part].astype(F32) + b[:, part].astype(F32)).astype(BF16)
        for m, to in enumerate((one_to, two_to, three_to, four_to)):
            going.append(copies.start(a.at[m * 32 : (m + 1) * 32, part], to.at[:, part]))
    finish(going)


def join_body(one_at, two_at, three_at, four_at, mini_at, out_to, pieces, mini, out, sems):
    copies = Copies(sems)
    coming = [
        [
            copies.start(at.at[:, columns_of(n)], pieces.at[m, :, columns_of(n)])
            for m, at in enumerate((one_at, two_at, three_at, four_at))
        ]
        for n in range(STEPS)
    ]
    last = copies.start(mini_at, mini)
    going = []
    for n in range(STEPS):
        part = columns_of(n)
        finish(coming[n])
        total = pieces[0, :, part].astype(F32) + pieces[1, :, part].astype(F32)
        total = total + pieces[2, :, part].astype(F32) + pieces[3, :, part].astype(F32)
        out[:, part] = total.astype(BF16)
        going.append(copies.start(out.at[:, part], out_to.at[:, part]))
    last.wait()
    total = mini[0].astype(F32)
    for n in range(1, mini.shape[0]):
        total = total + mini[n].astype(F32)
    out[:, MAIN:] = total.astype(BF16)
    going.append(copies.start(out.at[:, MAIN:], out_to.at[:, MAIN:]))
    finish(going)


def unpack_body(pieces, up, up_left, up_right, down, down_left, down_right):
    total = pieces[0].astype(F32)
    for n in range(1, pieces.shape[0]):
        total = total + pieces[n].astype(F32)
    top, low = total[:4].astype(BF16), total[4:].astype(BF16)
    total = total.astype(BF16)
    for b in range(BLOCKS):
        for k in range(FACTORS):
            at = (k // 2) * GROUP + b * SIDE
            up[k, b] = (low if k % 2 else top)[:, at : at + SIDE]
            at = DOWN_AT + (b * FACTORS + k) * ROWS
            down[k, b] = total[:, at : at + ROWS]
    up_right[...] = low[:, 2 * GROUP : 3 * GROUP]
    down_left[:, :SLAB] = top[:, LEFT_AT:MAIN]
    down_left[:, SLAB:] = low[:, LEFT_AT:MAIN]
    up_left[...] = top[:, MAIN:]
    down_right[...] = low[:, MAIN:]


SPACES = {"s": pltpu.SMEM, "v": pltpu.VMEM, "h": pltpu.HBM, "a": pl.ANY, "c": pl.ANY}


def call(body, outs, kinds, scratch=(), copies=0, cost=(0, 0), limit=LIMIT):
    kinds, kinds_out = kinds.split()
    sems = [pltpu.SemaphoreType.DMA((copies,))] if copies else []

    def run(*args):
        args = [
            pltpu.with_memory_space_constraint(a, pltpu.HBM) if k == "h" else a
            for a, k in zip(args, kinds)
        ]
        every = kinds + kinds_out
        shapes = [(a.shape, a.dtype) for a in args] + list(outs)
        staged = [pltpu.VMEM(*shapes[n]) for n, k in enumerate(every) if k == "c"]
        extra = [pltpu.SemaphoreType.DMA((len(staged),))] if staged else []

        def kernel(*refs):
            refs, rest = list(refs[: len(every)]), list(refs[len(every) :])
            if staged:
                buffers, rest = rest[: len(staged)], rest[len(staged) :]
                stage = Copies(rest.pop())
                places = [n for n, k in enumerate(every) if k == "c"]
                pairs = [(n, refs[n], buffer) for n, buffer in zip(places, buffers)]
                coming = [(o, u) for n, o, u in pairs if n < len(kinds)]
                going = [(u, o) for n, o, u in pairs if n >= len(kinds)]
                for n, _, buffer in pairs:
                    refs[n] = buffer
                started = [stage.start(*pair) for pair in coming]
                finish(started)
            body(*refs, *rest)
            if staged:
                finish([stage.start(*pair) for pair in going])

        return pl.pallas_call(
            kernel,
            out_shape=[jax.ShapeDtypeStruct(s, d) for s, d in outs],
            in_specs=[pl.BlockSpec(memory_space=SPACES[k]) for k in kinds],
            out_specs=[pl.BlockSpec(memory_space=SPACES[k]) for k in kinds_out],
            scratch_shapes=staged + [pltpu.VMEM(s, d) for s, d in scratch] + sems + extra,
            compiler_params=pltpu.CompilerParams(vmem_limit_bytes=limit),
            cost_estimate=pl.CostEstimate(
                flops=cost[0], bytes_accessed=cost[1], transcendentals=0
            ),
        )(*args)

    return run


def swap(block, axis, mask):
    count = lax.axis_size(axis)
    return lax.ppermute(block, axis, [(i, i ^ mask) for i in range(count)])


def exchange(block, axis):
    return lax.all_to_all(block, axis, 0, 0)


def all_sum(partial):
    count = SIZES[3] * SIZES[4]
    pieces = exchange(partial.reshape(count, ROWS // count, 2 * ROWS), TENSOR)
    piece = jnp.sum(pieces, axis=0).astype(BF16)
    return exchange(jnp.broadcast_to(piece, pieces.shape), TENSOR).reshape(ROWS, 2 * ROWS)


def body(tokens, cotangent, up_blocks, up_left, up_right, down_blocks, down_left, down_right):
    scale = 1.0 / math.sqrt(ROWS * SIZES[0] * SIZES[1] * SIZES[2])
    index = lax.axis_index
    place = jnp.stack([index("core"), index("x")]).astype(jnp.int32)
    wide, lows = (2 * ROWS, SLAB), (ROWS, 2 * ROWS)
    hops = (("y", 1), ("y", 2), ("zl", 1), ("zl", 2))
    shape = lambda a: (a.shape, a.dtype)

    own, low = call(
        low_body,
        [(wide, BF16), (lows, F32)],
        "hhhh cc",
        [shape(up_left), shape(down_right)],
        4,
        cost=(40_000_000, 2_000_000),
    )(tokens, cotangent, up_left, down_right)
    low = all_sum(low)
    arrived = [swap(own, axis, mask) for axis, mask in hops]

    half = (ROWS, MAIN)
    weights = (up_blocks, up_right, down_blocks, down_left)
    local, *terms, packed, keep, send = call(
        functools.partial(main_body, scale),
        [(wide, F32)] + [(wide, BF16)] * 4 + [((16, LOW, SLAB), BF16), (half, BF16), (half, BF16)],
        "saaaaaahhhh aaaaaaaa",
        [((FACTORS, *wide), BF16), shape(low)]
        + [shape(a) for a in weights]
        + [(wide, F32), ((FACTORS - 1, *wide), BF16), ((LOW, SLAB), BF16), (half, BF16), (half, BF16)],
        80,
        cost=(1_500_000_000, 10_000_000),
    )(place, own, *arrived, low, *weights)

    low = exchange(packed, TENSOR)
    got = swap(send, "core", 1)
    pieces = call(
        split_body,
        [((32, MAIN), BF16)] * 4,
        "aa aaaa",
        [(half, BF16)] * 2,
        6 * STEPS,
        cost=(30_000_000_000, 5_000_000),
    )(keep, got)
    pieces = list(pieces[:1]) + [swap(pieces[mask], "x", mask) for mask in (1, 2, 3)]
    far = [swap(term, axis, mask) for term, (axis, mask) in zip(terms[2:], hops[2:])]

    low, mini = call(
        functools.partial(mini_body, scale),
        [(lows, BF16), ((2 * ROWS, MINI), BF16)],
        "cc cc",
        cost=(40_000_000, 1_000_000),
    )(own, low)
    mini = exchange(mini.reshape(8, -1, MINI), ("x", "core"))

    pieces, far = lax.optimization_barrier((pieces, far))
    pieces = call(
        join_body,
        [((32, MAIN + MINI), BF16)],
        "aaaaa a",
        [((4, 32, MAIN), BF16), (mini.shape, BF16), ((32, MAIN + MINI), BF16)],
        5 * STEPS + 2,
        cost=(1_000_000, 2_000_000),
    )(*pieces, mini)[0]
    near, pieces, low = lax.optimization_barrier((terms[:2], pieces, low))
    pieces = exchange(pieces.reshape(SIZES[0], 8, -1), "zh")
    terms = [swap(term, axis, mask) for term, (axis, mask) in zip(near, hops[:2])] + far

    out, tokens_grad = call(
        last_body, [((ROWS, SLAB), BF16)] * 2, "cccccccc cc", cost=(40_000_000, 2_000_000)
    )(local, *terms, low, up_left, down_right)

    up_g, up_left_g, up_right_g, down_g, down_left_g, down_right_g = call(
        unpack_body,
        [
            ((FACTORS, BLOCKS, 4, SIDE), BF16),
            ((4, SLAB), BF16),
            ((4, HIDDEN), BF16),
            ((FACTORS, BLOCKS, 8, ROWS), BF16),
            ((4, HIDDEN), BF16),
            ((4, SLAB), BF16),
        ],
        "v cccccc",
        cost=(1_000_000, 1_000_000),
        limit=SMALL,
    )(pieces)
    return (out, tokens_grad, up_g, up_left_g.T, up_right_g, down_g, down_left_g.T, down_right_g)


def solution(mesh):
    fine = Mesh(mesh.devices.reshape(SIZES), DP + TENSOR)
    in_specs = (
        P(DP, TENSOR),
        P(DP, TENSOR),
        P(None, TENSOR, None, None),
        P(TENSOR, None),
        P(None, TENSOR),
        P(None, TENSOR, None, None),
        P(TENSOR, None),
        P(None, TENSOR),
    )
    out_specs = (
        P(DP, TENSOR),
        P(DP, TENSOR),
        P(None, TENSOR, DP, None),
        P(TENSOR, DP),
        P(DP, TENSOR),
        P(None, TENSOR, DP, None),
        P(TENSOR, DP),
        P(DP, TENSOR),
    )
    return jax.shard_map(body, mesh=fine, in_specs=in_specs, out_specs=out_specs, check_vma=False)
```

```python
import functools
import math

import jax
import jax.numpy as jnp
from jax import lax
from jax.experimental import pallas as pl
from jax.experimental.pallas import tpu as pltpu
from jax.sharding import Mesh
from jax.sharding import PartitionSpec as P

DP = ("zh", "x", "core")
TENSOR = ("zl", "y")
SIZES = (4, 4, 2, 4, 4)
ROWS = 128
SIDE = 256
SLAB = 512
HIDDEN = 1024
BLOCKS = 4
FACTORS = 5
F32 = jnp.float32
BF16 = jnp.bfloat16

GROUP = BLOCKS * SIDE
DOWN_AT = 3 * GROUP
LEFT_AT = DOWN_AT + BLOCKS * FACTORS * ROWS
MAIN = LEFT_AT + SLAB
MINI = SLAB
LOW = ROWS // 2
LIMIT = 63 * 1024 * 1024
SMALL = 16 * 1024 * 1024


def mm(a, b):
    return lax.dot_general(a, b, (((1,), (0,)), ((), ())), preferred_element_type=F32)


def mt(a, b):
    return lax.dot_general(a, b, (((1,), (1,)), ((), ())), preferred_element_type=F32)


def pick(place):
    core, x_here = place[0], place[1]
    row = lax.broadcasted_iota(jnp.int32, (SIDE, SIDE), 0)
    column = lax.broadcasted_iota(jnp.int32, (SIDE, SIDE), 1)
    quarter, half = row & 3, (row >> 2) & 1
    zh, x = (row >> 3) & 3, (row >> 5) & 3
    at = zh * 8 + (x ^ x_here) * 2 + ((row >> 7) ^ core)
    pair = (column == half * ROWS + at * 4 + quarter).astype(BF16)
    whole = (column == at * 8 + half * 4 + quarter).astype(BF16)
    return pair, whole


def pick_mini():
    row = lax.broadcasted_iota(jnp.int32, (SIDE, SIDE), 0)
    column = lax.broadcasted_iota(jnp.int32, (SIDE, SIDE), 1)
    quarter, half = row & 3, (row >> 2) & 1
    at = ((row >> 3) & 3) * 8 + (row >> 5)
    return (column == half * ROWS + at * 4 + quarter).astype(BF16)


class Copies:
    def __init__(self, sems):
        self.sems, self.count = sems, 0

    def start(self, source, target):
        copy = pltpu.make_async_copy(source, target, self.sems.at[self.count])
        self.count += 1
        copy.start()
        return copy


def finish(copies):
    for copy in copies:
        copy.wait()


def fold(low):
    return jnp.concatenate([low[:LOW], low[LOW:]], axis=1).astype(BF16)


def low_body(tokens, cotangent, up_left, down_right, own, low, u, d, sems):
    copies = Copies(sems)
    t, c = own.at[:ROWS], own.at[ROWS:]
    first = [copies.start(tokens, t), copies.start(up_left, u)]
    second = [copies.start(cotangent, c), copies.start(down_right, d)]
    finish(first)
    low[:, :ROWS] = mm(t[...], u[...])
    finish(second)
    low[:, ROWS:] = mt(c[...], d[...])


def main_body(
    scale, place, own_at, one_at, two_at, three_at, four_at, low_at, up_at, up_right_at, down_at, down_left_at,
    local_to, one_to, two_to, three_to, four_to, packed_to, keep_to, send_to,
    arrived, low, up, up_right, down, down_left, local, sent, packed, keep, send, sems,
):
    copies = Copies(sems)
    first = [
        copies.start(low_at, low),
        copies.start(up_right_at, up_right),
        copies.start(down_left_at, down_left),
    ]
    first += [
        copies.start(a, arrived.at[n])
        for n, a in enumerate((own_at, one_at, two_at, three_at, four_at))
    ]
    blocks = [
        (copies.start(up_at.at[:, b], up.at[:, b]), copies.start(down_at.at[:, b], down.at[:, b]))
        for b in range(BLOCKS)
    ]
    pair, whole = pick(place)
    out_going = []

    def put(at, value):
        value = (value * scale).astype(BF16)
        columns = slice(at, at + value.shape[1])
        keep[:, columns] = value[:ROWS]
        send[:, columns] = value[ROWS:]
        out_going.append(copies.start(send.at[:, columns], send_to.at[:, columns]))
        out_going.append(copies.start(keep.at[:, columns], keep_to.at[:, columns]))

    finish(first)
    low_up, low_cot = low[:, :ROWS], low[:, ROWS:]
    hiddens, pres = [], []
    low_down = jnp.zeros((ROWS, ROWS), F32)
    low_pre = jnp.zeros((ROWS, ROWS), F32)
    for b in range(BLOCKS):
        features = slice(b * ROWS, (b + 1) * ROWS)
        units = slice(b * SIDE, (b + 1) * SIDE)
        value = mm(low_up, up_right[:, units])
        grad = mt(low_cot, down_left[units, :])
        finish(blocks[b])
        for k in range(FACTORS):
            value = value + mm(arrived[k, :ROWS, features], up[k, b])
            grad = grad + mt(arrived[k, ROWS:, features], down[k, b])
        phi = 0.5 + 0.5 * lax.erf(value * math.sqrt(0.5))
        density = jnp.exp(-0.5 * value * value) * (1.0 / math.sqrt(2.0 * math.pi))
        hidden = (value * phi).astype(BF16)
        pre = (grad * (phi + value * density)).astype(BF16)
        hiddens.append(hidden)
        pres.append(pre)
        low_down = low_down + mm(hidden, down_left[units, :])
        low_pre = low_pre + mt(pre, up_right[:, units])
    packed[...] = fold(jnp.concatenate([low_down, low_pre], axis=1))
    out_going += [copies.start(packed, packed_to.at[n]) for n in range(packed_to.shape[0])]
    for b in range(BLOCKS):
        features = slice(b * ROWS, (b + 1) * ROWS)
        hidden, pre = hiddens[b], pres[b]
        for k in range(FACTORS):
            upper, lower = mm(hidden, down[k, b]), mt(pre, up[k, b])
            if k:
                sent[k - 1, :ROWS, features] = upper.astype(BF16)
                sent[k - 1, ROWS:, features] = lower.astype(BF16)
            else:
                local[:ROWS, features] = upper
                local[ROWS:, features] = lower
    for n, to in enumerate((one_to, two_to, three_to, four_to)):
        out_going.append(copies.start(sent.at[n], to))
    out_going.append(copies.start(local, local_to))
    for b in range(BLOCKS):
        features = slice(b * ROWS, (b + 1) * ROWS)
        hidden, pre = hiddens[b], pres[b]
        left = [arrived[k, :ROWS, features] for k in range(FACTORS)] + [low_up]
        cot = [arrived[k, ROWS:, features] for k in range(FACTORS)]
        for g in range(3):
            rows = jnp.concatenate([left[2 * g], left[2 * g + 1]], axis=1)
            put(g * GROUP + b * SIDE, mm(mt(pair, rows).astype(BF16), pre))
        rows = mt(whole, hidden).astype(BF16)
        put(DOWN_AT + b * FACTORS * ROWS, mm(rows, jnp.concatenate(cot, axis=1)))
    zero = jnp.zeros_like(low_cot)
    upper = mt(pair, jnp.concatenate([low_cot, zero], axis=1)).astype(BF16)
    lower = mt(pair, jnp.concatenate([zero, low_cot], axis=1)).astype(BF16)
    put(
        LEFT_AT,
        mm(upper, jnp.concatenate(hiddens[:2], axis=1))
        + mm(lower, jnp.concatenate(hiddens[2:], axis=1)),
    )
    finish(out_going)


def mini_body(scale, own_at, pieces_at, low, mini, own, pieces, sems):
    copies = Copies(sems)
    coming = [copies.start(pieces_at.at[n : n + 4], pieces.at[n : n + 4]) for n in range(0, pieces.shape[0], 4)]
    last = copies.start(own_at, own)
    pair = pick_mini()
    total = jnp.zeros((LOW, SLAB), F32)
    for n, copy in enumerate(coming):
        copy.wait()
        for m in range(4 * n, 4 * n + 4):
            total = total + pieces[m].astype(F32)
    total = total.astype(BF16)
    low_down = jnp.concatenate([total[:, :ROWS], total[:, 2 * ROWS : 3 * ROWS]], axis=0)
    low_pre = jnp.concatenate([total[:, ROWS : 2 * ROWS], total[:, 3 * ROWS :]], axis=0)
    low[:, :ROWS] = low_down
    low[:, ROWS:] = low_pre
    zero = jnp.zeros_like(low_pre)
    upper = mt(pair, jnp.concatenate([low_pre, zero], axis=1)).astype(BF16)
    lower = mt(pair, jnp.concatenate([zero, low_down], axis=1)).astype(BF16)
    last.wait()
    value = mm(upper, own[:ROWS, :]) + mm(lower, own[ROWS:, :])
    mini[...] = (value * scale).astype(BF16)


def last_body(local, one, two, three, four, low, up_left, down_right, out, grad):
    total = local[...]
    for a in (one, two, three, four):
        total = total + a[...].astype(F32)
    out[...] = (total[:ROWS] + mm(low[:, :ROWS], down_right[...])).astype(BF16)
    grad[...] = (total[ROWS:] + mt(low[:, ROWS:], up_left[...])).astype(BF16)


STEPS = 4


def columns_of(n):
    return slice(n * (MAIN // STEPS), (n + 1) * (MAIN // STEPS))


def split_body(a_at, b_at, one_to, two_to, three_to, four_to, a, b, sems):
    copies = Copies(sems)
    coming = [
        [copies.start(at.at[:, columns_of(n)], to.at[:, columns_of(n)]) for at, to in ((a_at, a), (b_at, b))]
        for n in range(STEPS)
    ]
    going = []
    for n in range(STEPS):
        part = columns_of(n)
        finish(coming[n])
        a[:, part] = (a[:, part].astype(F32) + b[:, part].astype(F32)).astype(BF16)
        for m, to in enumerate((one_to, two_to, three_to, four_to)):
            going.append(copies.start(a.at[m * 32 : (m + 1) * 32, part], to.at[:, part]))
    finish(going)


def join_body(one_at, two_at, three_at, four_at, mini_at, out_to, pieces, mini, out, sems):
    copies = Copies(sems)
    coming = [
        [
            copies.start(at.at[:, columns_of(n)], pieces.at[m, :, columns_of(n)])
            for m, at in enumerate((one_at, two_at, three_at, four_at))
        ]
        for n in range(STEPS)
    ]
    last = copies.start(mini_at, mini)
    going = []
    for n in range(STEPS):
        part = columns_of(n)
        finish(coming[n])
        total = pieces[0, :, part].astype(F32) + pieces[1, :, part].astype(F32)
        total = total + pieces[2, :, part].astype(F32) + pieces[3, :, part].astype(F32)
        out[:, part] = total.astype(BF16)
        going.append(copies.start(out.at[:, part], out_to.at[:, part]))
    last.wait()
    total = mini[0].astype(F32)
    for n in range(1, mini.shape[0]):
        total = total + mini[n].astype(F32)
    out[:, MAIN:] = total.astype(BF16)
    going.append(copies.start(out.at[:, MAIN:], out_to.at[:, MAIN:]))
    finish(going)


def unpack_body(pieces, up, up_left, up_right, down, down_left, down_right):
    total = pieces[0].astype(F32)
    for n in range(1, pieces.shape[0]):
        total = total + pieces[n].astype(F32)
    top, low = total[:4].astype(BF16), total[4:].astype(BF16)
    total = total.astype(BF16)
    for b in range(BLOCKS):
        for k in range(FACTORS):
            at = (k // 2) * GROUP + b * SIDE
            up[k, b] = (low if k % 2 else top)[:, at : at + SIDE]
            at = DOWN_AT + (b * FACTORS + k) * ROWS
            down[k, b] = total[:, at : at + ROWS]
    up_right[...] = low[:, 2 * GROUP : 3 * GROUP]
    down_left[:, :SLAB] = top[:, LEFT_AT:MAIN]
    down_left[:, SLAB:] = low[:, LEFT_AT:MAIN]
    up_left[...] = top[:, MAIN:]
    down_right[...] = low[:, MAIN:]


SPACES = {"s": pltpu.SMEM, "v": pltpu.VMEM, "h": pltpu.HBM, "a": pl.ANY, "c": pl.ANY}


def call(body, outs, kinds, scratch=(), copies=0, cost=(0, 0), limit=LIMIT):
    kinds, kinds_out = kinds.split()
    sems = [pltpu.SemaphoreType.DMA((copies,))] if copies else []

    def run(*args):
        args = [
            pltpu.with_memory_space_constraint(a, pltpu.HBM) if k == "h" else a
            for a, k in zip(args, kinds)
        ]
        every = kinds + kinds_out
        shapes = [(a.shape, a.dtype) for a in args] + list(outs)
        staged = [pltpu.VMEM(*shapes[n]) for n, k in enumerate(every) if k == "c"]
        extra = [pltpu.SemaphoreType.DMA((len(staged),))] if staged else []

        def kernel(*refs):
            refs, rest = list(refs[: len(every)]), list(refs[len(every) :])
            if staged:
                buffers, rest = rest[: len(staged)], rest[len(staged) :]
                stage = Copies(rest.pop())
                places = [n for n, k in enumerate(every) if k == "c"]
                pairs = [(n, refs[n], buffer) for n, buffer in zip(places, buffers)]
                coming = [(o, u) for n, o, u in pairs if n < len(kinds)]
                going = [(u, o) for n, o, u in pairs if n >= len(kinds)]
                for n, _, buffer in pairs:
                    refs[n] = buffer
                started = [stage.start(*pair) for pair in coming]
                finish(started)
            body(*refs, *rest)
            if staged:
                finish([stage.start(*pair) for pair in going])

        return pl.pallas_call(
            kernel,
            out_shape=[jax.ShapeDtypeStruct(s, d) for s, d in outs],
            in_specs=[pl.BlockSpec(memory_space=SPACES[k]) for k in kinds],
            out_specs=[pl.BlockSpec(memory_space=SPACES[k]) for k in kinds_out],
            scratch_shapes=staged + [pltpu.VMEM(s, d) for s, d in scratch] + sems + extra,
            compiler_params=pltpu.CompilerParams(vmem_limit_bytes=limit),
            cost_estimate=pl.CostEstimate(
                flops=cost[0], bytes_accessed=cost[1], transcendentals=0
            ),
        )(*args)

    return run


def swap(block, axis, mask):
    count = lax.axis_size(axis)
    return lax.ppermute(block, axis, [(i, i ^ mask) for i in range(count)])


def exchange(block, axis):
    return lax.all_to_all(block, axis, 0, 0)


def all_sum(partial):
    count = SIZES[3] * SIZES[4]
    pieces = exchange(partial.reshape(count, ROWS // count, 2 * ROWS), TENSOR)
    piece = jnp.sum(pieces, axis=0).astype(BF16)
    return exchange(jnp.broadcast_to(piece, pieces.shape), TENSOR).reshape(ROWS, 2 * ROWS)


def body(tokens, cotangent, up_blocks, up_left, up_right, down_blocks, down_left, down_right):
    scale = 1.0 / math.sqrt(ROWS * SIZES[0] * SIZES[1] * SIZES[2])
    index = lax.axis_index
    place = jnp.stack([index("core"), index("x")]).astype(jnp.int32)
    wide, lows = (2 * ROWS, SLAB), (ROWS, 2 * ROWS)
    hops = (("y", 1), ("y", 2), ("zl", 1), ("zl", 2))
    shape = lambda a: (a.shape, a.dtype)

    own, low = call(
        low_body,
        [(wide, BF16), (lows, F32)],
        "hhhh cc",
        [shape(up_left), shape(down_right)],
        4,
        cost=(40_000_000, 2_000_000),
    )(tokens, cotangent, up_left, down_right)
    low = all_sum(low)
    arrived = [swap(own, axis, mask) for axis, mask in hops]

    half = (ROWS, MAIN)
    weights = (up_blocks, up_right, down_blocks, down_left)
    local, *terms, packed, keep, send = call(
        functools.partial(main_body, scale),
        [(wide, F32)] + [(wide, BF16)] * 4 + [((16, LOW, SLAB), BF16), (half, BF16), (half, BF16)],
        "saaaaaahhhh aaaaaaaa",
        [((FACTORS, *wide), BF16), shape(low)]
        + [shape(a) for a in weights]
        + [(wide, F32), ((FACTORS - 1, *wide), BF16), ((LOW, SLAB), BF16), (half, BF16), (half, BF16)],
        80,
        cost=(1_500_000_000, 10_000_000),
    )(place, own, *arrived, low, *weights)

    low = exchange(packed, TENSOR)
    got = swap(send, "core", 1)
    pieces = call(
        split_body,
        [((32, MAIN), BF16)] * 4,
        "ha aaaa",
        [(half, BF16)] * 2,
        6 * STEPS,
        cost=(30_000_000_000, 5_000_000),
        limit=SMALL,
    )(keep, got)
    two_off = swap(pieces[2], "x", 2)
    pieces = [pieces[0], two_off] + [swap(pieces[mask], "x", mask) for mask in (1, 3)]
    far = [swap(term, axis, mask) for term, (axis, mask) in zip(terms[2:], hops[2:])]

    low, mini = call(
        functools.partial(mini_body, scale),
        [(lows, BF16), ((2 * ROWS, MINI), BF16)],
        "aa cc",
        [shape(own), shape(low)],
        5,
        cost=(40_000_000, 1_000_000),
    )(own, low)
    mini = exchange(mini.reshape(8, -1, MINI), ("x", "core"))

    pieces, far = lax.optimization_barrier((pieces, far))
    pieces = call(
        join_body,
        [((32, MAIN + MINI), BF16)],
        "aaaaa a",
        [((4, 32, MAIN), BF16), (mini.shape, BF16), ((32, MAIN + MINI), BF16)],
        5 * STEPS + 2,
        cost=(1_000_000, 2_000_000),
        limit=SMALL,
    )(*pieces, mini)[0]
    near, pieces, low = lax.optimization_barrier((terms[:2], pieces, low))
    pieces = exchange(pieces.reshape(SIZES[0], 8, -1), "zh")
    terms = [swap(term, axis, mask) for term, (axis, mask) in zip(near, hops[:2])] + far

    out, tokens_grad = call(
        last_body, [((ROWS, SLAB), BF16)] * 2, "cccccccc cc", cost=(40_000_000, 2_000_000)
    )(local, *terms, low, up_left, down_right)

    up_g, up_left_g, up_right_g, down_g, down_left_g, down_right_g = call(
        unpack_body,
        [
            ((FACTORS, BLOCKS, 4, SIDE), BF16),
            ((4, SLAB), BF16),
            ((4, HIDDEN), BF16),
            ((FACTORS, BLOCKS, 8, ROWS), BF16),
            ((4, HIDDEN), BF16),
            ((4, SLAB), BF16),
        ],
        "v cccccc",
        cost=(1_000_000, 1_000_000),
        limit=SMALL,
    )(pieces)
    return (out, tokens_grad, up_g, up_left_g.T, up_right_g, down_g, down_left_g.T, down_right_g)


def solution(mesh):
    fine = Mesh(mesh.devices.reshape(SIZES), DP + TENSOR)
    in_specs = (
        P(DP, TENSOR),
        P(DP, TENSOR),
        P(None, TENSOR, None, None),
        P(TENSOR, None),
        P(None, TENSOR),
        P(None, TENSOR, None, None),
        P(TENSOR, None),
        P(None, TENSOR),
    )
    out_specs = (
        P(DP, TENSOR),
        P(DP, TENSOR),
        P(None, TENSOR, DP, None),
        P(TENSOR, DP),
        P(DP, TENSOR),
        P(None, TENSOR, DP, None),
        P(TENSOR, DP),
        P(DP, TENSOR),
    )
    return jax.shard_map(body, mesh=fine, in_specs=in_specs, out_specs=out_specs, check_vma=False)
```

```python
import functools
import math

import jax
import jax.numpy as jnp
from jax import lax
from jax.experimental import pallas as pl
from jax.experimental.pallas import tpu as pltpu
from jax.sharding import Mesh
from jax.sharding import PartitionSpec as P

DP = ("zh", "x", "core")
TENSOR = ("zl", "y")
SIZES = (4, 4, 2, 4, 4)
ROWS = 128
SIDE = 256
SLAB = 512
HIDDEN = 1024
BLOCKS = 4
FACTORS = 5
F32 = jnp.float32
BF16 = jnp.bfloat16

GROUP = BLOCKS * SIDE
DOWN_AT = 3 * GROUP
LEFT_AT = DOWN_AT + BLOCKS * FACTORS * ROWS
MAIN = LEFT_AT + SLAB
MINI = SLAB
LOW = ROWS // 2
LIMIT = 63 * 1024 * 1024
SMALL = 16 * 1024 * 1024


def mm(a, b):
    return lax.dot_general(a, b, (((1,), (0,)), ((), ())), preferred_element_type=F32)


def mt(a, b):
    return lax.dot_general(a, b, (((1,), (1,)), ((), ())), preferred_element_type=F32)


def pick(place):
    core, x_here = place[0], place[1]
    row = lax.broadcasted_iota(jnp.int32, (SIDE, SIDE), 0)
    column = lax.broadcasted_iota(jnp.int32, (SIDE, SIDE), 1)
    quarter, half = row & 3, (row >> 2) & 1
    zh, x = (row >> 3) & 3, (row >> 5) & 3
    at = zh * 8 + (x ^ x_here) * 2 + ((row >> 7) ^ core)
    pair = (column == half * ROWS + at * 4 + quarter).astype(BF16)
    whole = (column == at * 8 + half * 4 + quarter).astype(BF16)
    return pair, whole


def pick_mini():
    row = lax.broadcasted_iota(jnp.int32, (SIDE, SIDE), 0)
    column = lax.broadcasted_iota(jnp.int32, (SIDE, SIDE), 1)
    quarter, half = row & 3, (row >> 2) & 1
    at = ((row >> 3) & 3) * 8 + (row >> 5)
    return (column == half * ROWS + at * 4 + quarter).astype(BF16)


class Copies:
    def __init__(self, sems):
        self.sems, self.count = sems, 0

    def start(self, source, target):
        copy = pltpu.make_async_copy(source, target, self.sems.at[self.count])
        self.count += 1
        copy.start()
        return copy


def finish(copies):
    for copy in copies:
        copy.wait()


def fold(low):
    return jnp.concatenate([low[:LOW], low[LOW:]], axis=1).astype(BF16)


def unfold(pieces):
    total = pieces[0].astype(F32)
    for n in range(1, pieces.shape[0]):
        total = total + pieces[n].astype(F32)
    total = total.astype(BF16)
    first = jnp.concatenate([total[:, :ROWS], total[:, 2 * ROWS : 3 * ROWS]], axis=0)
    second = jnp.concatenate([total[:, ROWS : 2 * ROWS], total[:, 3 * ROWS :]], axis=0)
    return first, second


def low_body(tokens, cotangent, up_left, down_right, own, low, u, d, sems):
    copies = Copies(sems)
    t, c = own.at[:ROWS], own.at[ROWS:]
    first = [copies.start(tokens, t), copies.start(up_left, u)]
    second = [copies.start(cotangent, c), copies.start(down_right, d)]
    finish(first)
    low[:, :ROWS] = mm(t[...], u[...])
    finish(second)
    low[:, ROWS:] = mt(c[...], d[...])


def main_body(
    scale, place, own_at, one_at, two_at, three_at, four_at, low_at, up_at, up_right_at, down_at, down_left_at,
    local_to, one_to, two_to, three_to, four_to, packed_to, keep_to, send_to,
    arrived, low, up, up_right, down, down_left, local, sent, packed, keep, send, sems,
):
    copies = Copies(sems)
    first = [
        copies.start(low_at, low),
        copies.start(up_right_at, up_right),
        copies.start(down_left_at, down_left),
    ]
    first += [
        copies.start(a, arrived.at[n])
        for n, a in enumerate((own_at, one_at, two_at, three_at, four_at))
    ]
    blocks = [
        (copies.start(up_at.at[:, b], up.at[:, b]), copies.start(down_at.at[:, b], down.at[:, b]))
        for b in range(BLOCKS)
    ]
    pair, whole = pick(place)
    out_going = []

    def put(at, value):
        value = (value * scale).astype(BF16)
        columns = slice(at, at + value.shape[1])
        keep[:, columns] = value[:ROWS]
        send[:, columns] = value[ROWS:]
        out_going.append(copies.start(send.at[:, columns], send_to.at[:, columns]))
        out_going.append(copies.start(keep.at[:, columns], keep_to.at[:, columns]))

    finish(first)
    low_up, low_cot = low[:, :ROWS], low[:, ROWS:]
    hiddens, pres = [], []
    low_down = jnp.zeros((ROWS, ROWS), F32)
    low_pre = jnp.zeros((ROWS, ROWS), F32)
    for b in range(BLOCKS):
        features = slice(b * ROWS, (b + 1) * ROWS)
        units = slice(b * SIDE, (b + 1) * SIDE)
        value = mm(low_up, up_right[:, units])
        grad = mt(low_cot, down_left[units, :])
        finish(blocks[b])
        for k in range(FACTORS):
            value = value + mm(arrived[k, :ROWS, features], up[k, b])
            grad = grad + mt(arrived[k, ROWS:, features], down[k, b])
        phi = 0.5 + 0.5 * lax.erf(value * math.sqrt(0.5))
        density = jnp.exp(-0.5 * value * value) * (1.0 / math.sqrt(2.0 * math.pi))
        hidden = (value * phi).astype(BF16)
        pre = (grad * (phi + value * density)).astype(BF16)
        hiddens.append(hidden)
        pres.append(pre)
        low_down = low_down + mm(hidden, down_left[units, :])
        low_pre = low_pre + mt(pre, up_right[:, units])
    packed[...] = fold(jnp.concatenate([low_down, low_pre], axis=1))
    out_going += [copies.start(packed, packed_to.at[n]) for n in range(4)]
    for b in range(BLOCKS):
        features = slice(b * ROWS, (b + 1) * ROWS)
        hidden, pre = hiddens[b], pres[b]
        for k in range(FACTORS):
            upper, lower = mm(hidden, down[k, b]), mt(pre, up[k, b])
            if k:
                sent[k - 1, :ROWS, features] = upper.astype(BF16)
                sent[k - 1, ROWS:, features] = lower.astype(BF16)
            else:
                local[:ROWS, features] = upper
                local[ROWS:, features] = lower
    for n, to in enumerate((one_to, two_to, three_to, four_to)):
        out_going.append(copies.start(sent.at[n], to))
    out_going.append(copies.start(local, local_to))
    for b in range(BLOCKS):
        features = slice(b * ROWS, (b + 1) * ROWS)
        hidden, pre = hiddens[b], pres[b]
        left = [arrived[k, :ROWS, features] for k in range(FACTORS)] + [low_up]
        cot = [arrived[k, ROWS:, features] for k in range(FACTORS)]
        for g in range(3):
            rows = jnp.concatenate([left[2 * g], left[2 * g + 1]], axis=1)
            put(g * GROUP + b * SIDE, mm(mt(pair, rows).astype(BF16), pre))
        rows = mt(whole, hidden).astype(BF16)
        put(DOWN_AT + b * FACTORS * ROWS, mm(rows, jnp.concatenate(cot, axis=1)))
    zero = jnp.zeros_like(low_cot)
    upper = mt(pair, jnp.concatenate([low_cot, zero], axis=1)).astype(BF16)
    lower = mt(pair, jnp.concatenate([zero, low_cot], axis=1)).astype(BF16)
    put(
        LEFT_AT,
        mm(upper, jnp.concatenate(hiddens[:2], axis=1))
        + mm(lower, jnp.concatenate(hiddens[2:], axis=1)),
    )
    finish(out_going)


def spread_body(pieces, out):
    total = pieces[0].astype(F32)
    for n in range(1, 4):
        total = total + pieces[n].astype(F32)
    total = total.astype(BF16)
    for n in range(4):
        out[n] = total


def mini_body(scale, own_at, pieces_at, low, mini, own, pieces, sems):
    copies = Copies(sems)
    first = copies.start(pieces_at, pieces)
    last = copies.start(own_at, own)
    pair = pick_mini()
    first.wait()
    low_down, low_pre = unfold(pieces)
    low[:, :ROWS] = low_down
    low[:, ROWS:] = low_pre
    zero = jnp.zeros_like(low_pre)
    upper = mt(pair, jnp.concatenate([low_pre, zero], axis=1)).astype(BF16)
    lower = mt(pair, jnp.concatenate([zero, low_down], axis=1)).astype(BF16)
    last.wait()
    value = mm(upper, own[:ROWS, :]) + mm(lower, own[ROWS:, :])
    mini[...] = (value * scale).astype(BF16)


def last_body(local, one, two, three, four, low, up_left, down_right, out, grad):
    total = local[...]
    for a in (one, two, three, four):
        total = total + a[...].astype(F32)
    out[...] = (total[:ROWS] + mm(low[:, :ROWS], down_right[...])).astype(BF16)
    grad[...] = (total[ROWS:] + mt(low[:, ROWS:], up_left[...])).astype(BF16)


STEPS = 4


def columns_of(n):
    return slice(n * (MAIN // STEPS), (n + 1) * (MAIN // STEPS))


def split_body(a_at, b_at, one_to, two_to, three_to, four_to, a, b, sems):
    copies = Copies(sems)
    coming = [
        [copies.start(at.at[:, columns_of(n)], to.at[:, columns_of(n)]) for at, to in ((a_at, a), (b_at, b))]
        for n in range(STEPS)
    ]
    going = []
    for n in range(STEPS):
        part = columns_of(n)
        finish(coming[n])
        a[:, part] = (a[:, part].astype(F32) + b[:, part].astype(F32)).astype(BF16)
        for m, to in enumerate((one_to, two_to, three_to, four_to)):
            going.append(copies.start(a.at[m * 32 : (m + 1) * 32, part], to.at[:, part]))
    finish(going)


def join_body(one_at, two_at, three_at, four_at, mini_at, out_to, pieces, mini, out, sems):
    copies = Copies(sems)
    coming = [
        [
            copies.start(at.at[:, columns_of(n)], pieces.at[m, :, columns_of(n)])
            for m, at in enumerate((one_at, two_at, three_at, four_at))
        ]
        for n in range(STEPS)
    ]
    last = copies.start(mini_at, mini)
    going = []
    for n in range(STEPS):
        part = columns_of(n)
        finish(coming[n])
        total = pieces[0, :, part].astype(F32) + pieces[1, :, part].astype(F32)
        total = total + pieces[2, :, part].astype(F32) + pieces[3, :, part].astype(F32)
        out[:, part] = total.astype(BF16)
        going.append(copies.start(out.at[:, part], out_to.at[:, part]))
    last.wait()
    total = mini[0].astype(F32)
    for n in range(1, mini.shape[0]):
        total = total + mini[n].astype(F32)
    out[:, MAIN:] = total.astype(BF16)
    going.append(copies.start(out.at[:, MAIN:], out_to.at[:, MAIN:]))
    finish(going)


def unpack_body(pieces, up, up_left, up_right, down, down_left, down_right):
    total = pieces[0].astype(F32)
    for n in range(1, pieces.shape[0]):
        total = total + pieces[n].astype(F32)
    top, low = total[:4].astype(BF16), total[4:].astype(BF16)
    total = total.astype(BF16)
    for b in range(BLOCKS):
        for k in range(FACTORS):
            at = (k // 2) * GROUP + b * SIDE
            up[k, b] = (low if k % 2 else top)[:, at : at + SIDE]
            at = DOWN_AT + (b * FACTORS + k) * ROWS
            down[k, b] = total[:, at : at + ROWS]
    up_right[...] = low[:, 2 * GROUP : 3 * GROUP]
    down_left[:, :SLAB] = top[:, LEFT_AT:MAIN]
    down_left[:, SLAB:] = low[:, LEFT_AT:MAIN]
    up_left[...] = top[:, MAIN:]
    down_right[...] = low[:, MAIN:]


SPACES = {"s": pltpu.SMEM, "v": pltpu.VMEM, "h": pltpu.HBM, "a": pl.ANY, "c": pl.ANY}


def call(body, outs, kinds, scratch=(), copies=0, cost=(0, 0), limit=LIMIT):
    kinds, kinds_out = kinds.split(" ")
    sems = [pltpu.SemaphoreType.DMA((copies,))] if copies else []

    def run(*args):
        args = [
            pltpu.with_memory_space_constraint(a, pltpu.HBM) if k == "h" else a
            for a, k in zip(args, kinds)
        ]
        every = kinds + kinds_out
        shapes = [(a.shape, a.dtype) for a in args] + list(outs)
        staged = [pltpu.VMEM(*shapes[n]) for n, k in enumerate(every) if k == "c"]
        extra = [pltpu.SemaphoreType.DMA((len(staged),))] if staged else []

        def kernel(*refs):
            refs, rest = list(refs[: len(every)]), list(refs[len(every) :])
            if staged:
                buffers, rest = rest[: len(staged)], rest[len(staged) :]
                stage = Copies(rest.pop())
                places = [n for n, k in enumerate(every) if k == "c"]
                pairs = [(n, refs[n], buffer) for n, buffer in zip(places, buffers)]
                coming = [(o, u) for n, o, u in pairs if n < len(kinds)]
                going = [(u, o) for n, o, u in pairs if n >= len(kinds)]
                for n, _, buffer in pairs:
                    refs[n] = buffer
                started = [stage.start(*pair) for pair in coming]
                finish(started)
            body(*refs, *rest)
            if staged:
                finish([stage.start(*pair) for pair in going])

        return pl.pallas_call(
            kernel,
            out_shape=[jax.ShapeDtypeStruct(s, d) for s, d in outs],
            in_specs=[pl.BlockSpec(memory_space=SPACES[k]) for k in kinds],
            out_specs=[pl.BlockSpec(memory_space=SPACES[k]) for k in kinds_out],
            scratch_shapes=staged + [pltpu.VMEM(s, d) for s, d in scratch] + sems + extra,
            compiler_params=pltpu.CompilerParams(vmem_limit_bytes=limit),
            cost_estimate=pl.CostEstimate(
                flops=cost[0], bytes_accessed=cost[1], transcendentals=0
            ),
        )(*args)

    return run


def swap(block, axis, mask):
    count = lax.axis_size(axis)
    return lax.ppermute(block, axis, [(i, i ^ mask) for i in range(count)])


def exchange(block, axis):
    return lax.all_to_all(block, axis, 0, 0)


def all_sum(partial):
    count = SIZES[3] * SIZES[4]
    pieces = exchange(partial.reshape(count, ROWS // count, 2 * ROWS), TENSOR)
    piece = jnp.sum(pieces, axis=0).astype(BF16)
    return exchange(jnp.broadcast_to(piece, pieces.shape), TENSOR).reshape(ROWS, 2 * ROWS)


def body(tokens, cotangent, up_blocks, up_left, up_right, down_blocks, down_left, down_right):
    scale = 1.0 / math.sqrt(ROWS * SIZES[0] * SIZES[1] * SIZES[2])
    index = lax.axis_index
    place = jnp.stack([index("core"), index("x")]).astype(jnp.int32)
    wide, lows = (2 * ROWS, SLAB), (ROWS, 2 * ROWS)
    hops = (("y", 1), ("y", 2), ("zl", 1), ("zl", 2))
    shape = lambda a: (a.shape, a.dtype)

    own, low = call(
        low_body,
        [(wide, BF16), (lows, F32)],
        "hhhh cc",
        [shape(up_left), shape(down_right)],
        4,
        cost=(40_000_000, 2_000_000),
    )(tokens, cotangent, up_left, down_right)
    low = all_sum(low)
    arrived = [swap(own, axis, mask) for axis, mask in hops]

    half = (ROWS, MAIN)
    weights = (up_blocks, up_right, down_blocks, down_left)
    local, *terms, packed, keep, send = call(
        functools.partial(main_body, scale),
        [(wide, F32)] + [(wide, BF16)] * 4 + [((4, LOW, SLAB), BF16), (half, BF16), (half, BF16)],
        "saaaaaahhhh aaaaaaaa",
        [((FACTORS, *wide), BF16), shape(low)]
        + [shape(a) for a in weights]
        + [(wide, F32), ((FACTORS - 1, *wide), BF16), ((LOW, SLAB), BF16), (half, BF16), (half, BF16)],
        80,
        cost=(1_500_000_000, 10_000_000),
    )(place, own, *arrived, low, *weights)

    low = exchange(packed, "y")
    got = swap(send, "core", 1)
    pieces = call(
        split_body,
        [((32, MAIN), BF16)] * 4,
        "ha aaaa",
        [(half, BF16)] * 2,
        6 * STEPS,
        cost=(30_000_000_000, 5_000_000),
        limit=SMALL,
    )(keep, got)
    low, terms, pieces = lax.optimization_barrier((low, terms, pieces))
    low = call(spread_body, [(low.shape, BF16)], "v v", cost=(30_000_000_000, 500_000), limit=SMALL)(low)[0]
    low = exchange(low, "zl")
    two_off = swap(pieces[2], "x", 2)
    pieces = [pieces[0], two_off] + [swap(pieces[mask], "x", mask) for mask in (1, 3)]
    far = [swap(term, axis, mask) for term, (axis, mask) in zip(terms[2:], hops[2:])]

    low, mini = call(
        functools.partial(mini_body, scale),
        [(lows, BF16), ((2 * ROWS, MINI), BF16)],
        "aa cc",
        [shape(own), shape(low)],
        2,
        cost=(40_000_000, 1_000_000),
    )(own, low)
    mini = exchange(mini.reshape(8, -1, MINI), ("x", "core"))

    pieces, far = lax.optimization_barrier((pieces, far))
    pieces = call(
        join_body,
        [((32, MAIN + MINI), BF16)],
        "aaaaa a",
        [((4, 32, MAIN), BF16), (mini.shape, BF16), ((32, MAIN + MINI), BF16)],
        5 * STEPS + 2,
        cost=(1_000_000, 2_000_000),
        limit=SMALL,
    )(*pieces, mini)[0]
    near, pieces, low = lax.optimization_barrier((terms[:2], pieces, low))
    pieces = exchange(pieces.reshape(SIZES[0], 8, -1), "zh")
    terms = [swap(term, axis, mask) for term, (axis, mask) in zip(near, hops[:2])] + far

    out, tokens_grad = call(
        last_body, [((ROWS, SLAB), BF16)] * 2, "cccccccc cc", cost=(40_000_000, 2_000_000)
    )(local, *terms, low, up_left, down_right)

    up_g, up_left_g, up_right_g, down_g, down_left_g, down_right_g = call(
        unpack_body,
        [
            ((FACTORS, BLOCKS, 4, SIDE), BF16),
            ((4, SLAB), BF16),
            ((4, HIDDEN), BF16),
            ((FACTORS, BLOCKS, 8, ROWS), BF16),
            ((4, HIDDEN), BF16),
            ((4, SLAB), BF16),
        ],
        "v cccccc",
        cost=(1_000_000, 1_000_000),
        limit=SMALL,
    )(pieces)
    return (out, tokens_grad, up_g, up_left_g.T, up_right_g, down_g, down_left_g.T, down_right_g)


def solution(mesh):
    fine = Mesh(mesh.devices.reshape(SIZES), DP + TENSOR)
    in_specs = (
        P(DP, TENSOR),
        P(DP, TENSOR),
        P(None, TENSOR, None, None),
        P(TENSOR, None),
        P(None, TENSOR),
        P(None, TENSOR, None, None),
        P(TENSOR, None),
        P(None, TENSOR),
    )
    out_specs = (
        P(DP, TENSOR),
        P(DP, TENSOR),
        P(None, TENSOR, DP, None),
        P(TENSOR, DP),
        P(DP, TENSOR),
        P(None, TENSOR, DP, None),
        P(TENSOR, DP),
        P(DP, TENSOR),
    )
    return jax.shard_map(body, mesh=fine, in_specs=in_specs, out_specs=out_specs, check_vma=False)
```
